1024 devices in a mesh: kx: 32 (over x_hi, y, core), ky: 32 (over x_lo, z).
Axes of the slice: x: 4 (x_hi: 2, x_lo: 2; x = x_hi * 2 + x_lo), y: 8, z: 16, core: 2. Of those that a mesh axis runs over, the one named last changes fastest.
Arguments:
- block: bfloat16 [32, 32, 2, 2, 128, 128], P('kx', 'ky'), may hold values from -4 to 4
- history: bfloat16 [32, 32, 2, 2, 128, 128], P('kx', 'ky'), may hold values from -0.5 to 0.5
Outputs:
- collision: float32 [32, 32, 2, 2, 128, 128], P('kx', 'ky')
The draws below stay inside these ranges and needn't reach their ends.
All inputs are finite; a program needn't handle non-finite values.
Results may differ from the reference program's by a relative error of at most 0.028.
Values may be sent and summed in bfloat16 or wider, within the bound.
A program may use at most 32 MiB of HBM per device.

```python
import math
import jax
import jax.numpy as jnp
from jax import lax

NKX = 32
NKY = 32
R = 128
H = 128
ITERS = 2


def block_levels(rng, dims, pieces, low, top_value):
    loudness = 1.0
    for dim, parts in pieces:
        draws = jax.random.uniform(jax.random.fold_in(jax.random.fold_in(rng, 6), dim), (parts,), jnp.float32, low / len(pieces), top_value / len(pieces))
        loudness = loudness * jnp.repeat(jnp.exp(draws), dims[dim] // parts).reshape((-1,) + (1,) * (len(dims) - 1 - dim))
    return loudness


def centred(rng, shape, deviation, most, cuts=(), kind=jnp.bfloat16):
    factor_of = block_levels(rng, shape, cuts, -0.22, 0.18) if cuts else 1.0
    result = jax.random.normal(rng, shape, jnp.float32) * deviation * factor_of
    return jnp.minimum(jnp.maximum(result, -most), most).astype(kind)


def setup_inputs(seed: int = 0) -> dict:
    splits = jax.random.split(jax.random.key(seed), 3)
    block = centred(splits[0], (NKX, NKY, 2, 2, R, H), 0.6, 4.0, ((0, 32), (1, 32)))
    history = centred(splits[1], (NKX, NKY, 2, 2, H, H), H ** -0.5, 0.5, ((0, 32), (1, 32)))
    return {"block": block, "history": history}


coupling = 0.5

def mirror(field):
    return jnp.roll(jnp.flip(field, (0, 1)), (1, 1), (0, 1))

def self_row(time_row):
    scale_all = math.sqrt(NKX * NKY)
    greens = lax.complex(time_row[:, :, :, 0], time_row[:, :, :, 1])
    site_green = jnp.fft.ifft2(greens, axes=(0, 1)) * scale_all
    retarded = site_green[:, :, 0]
    lesser = site_green[:, :, 1]
    self_ret = retarded * retarded * jnp.conj(mirror(lesser))
    self_les = lesser * lesser * jnp.conj(mirror(retarded))
    site_self = jnp.stack((self_ret, self_les), 2)
    rounded = jnp.stack((jnp.real(site_self), jnp.imag(site_self)), 3).astype(jnp.bfloat16)
    widened = lax.optimization_barrier(rounded).astype(jnp.float32)
    momentum_self = jnp.fft.fft2(lax.complex(widened[:, :, :, 0], widened[:, :, :, 1]), axes=(0, 1)) / scale_all
    return jnp.stack((jnp.real(momentum_self), jnp.imag(momentum_self)), 3).astype(jnp.bfloat16)

def matrix_product(left, right):
    return jnp.dot(left, right, preferred_element_type=jnp.float32)

def complex_product(left_real, left_imag, right_real, right_imag):
    real_out = matrix_product(left_real, right_real) - matrix_product(left_imag, right_imag)
    imag_out = matrix_product(left_real, right_imag) + matrix_product(left_imag, right_real)
    return (real_out, imag_out)

def collide(self_energy, history_local):
    adv_real = history_local[0, 0].T
    adv_imag = -history_local[0, 1].T
    ret_real, ret_imag = complex_product(self_energy[0, 0], self_energy[0, 1], history_local[0, 0], history_local[0, 1])
    first_real, first_imag = complex_product(self_energy[0, 0], self_energy[0, 1], history_local[1, 0], history_local[1, 1])
    second_real, second_imag = complex_product(self_energy[1, 0], self_energy[1, 1], adv_real, adv_imag)
    retarded = jnp.stack((ret_real, ret_imag), 0)
    lesser = jnp.stack((first_real + second_real, first_imag + second_imag), 0)
    return jnp.stack((retarded, lesser), 0)

def reference(block, history):
    current = block
    flat_history = history.reshape(NKX * NKY, 2, 2, H, H)
    collision = jnp.zeros((NKX, NKY, 2, 2, R, H), jnp.float32)
    for iteration in range(ITERS):
        by_rows = jnp.moveaxis(current.astype(jnp.float32), 4, 0)
        self_rows = lax.map(self_row, by_rows)
        momentum_self = jnp.moveaxis(self_rows, 0, 4).reshape(NKX * NKY, 2, 2, R, H)
        collision = lax.map(lambda operands: collide(operands[0], operands[1]), (momentum_self, flat_history))
        collision = collision.reshape(NKX, NKY, 2, 2, R, H)
        if iteration + 1 < ITERS:
            current = (block.astype(jnp.float32) + coupling * collision).astype(jnp.bfloat16)
    return collision
```

```python
import math

import jax
import jax.numpy as jnp
import numpy as np
from jax import lax
from jax.experimental import pallas as pl
from jax.experimental.pallas import tpu as pltpu
from jax.sharding import PartitionSpec as P

ITERS = 2
PHASES = 4
WIDE = 128

coupling = 0.5


def tables(n):
    q = WIDE // n
    spread = np.zeros((2 * WIDE, 2 * WIDE), np.float32)
    for j in range(n):
        for c in range(2):
            for i in range(q):
                spread[j * 2 * q + c * q + i, c * WIDE + i * n + j] = 1.0
    phases = np.outer(np.arange(n), np.arange(n)) % n * (2.0 * math.pi / n)
    cosine = np.cos(phases) / math.sqrt(n)
    sine = np.sin(phases) / math.sqrt(n)
    mixed = np.stack((np.stack((cosine, sine), 1), np.stack((-sine, cosine), 1)), 1)
    to_site = np.einsum("kcdx,ij->kcidxj", mixed, np.eye(q)).reshape(2 * WIDE, 2 * WIDE)
    back = (-np.arange(n)) % n
    forward = to_site.T.reshape(2, n, q, 2 * WIDE)
    mirrored = forward[:, back].reshape(2 * WIDE, 2 * WIDE)
    flip = np.einsum("xy,ij->xiyj", np.eye(n)[back], np.eye(q)).reshape(WIDE, WIDE)
    parts = (spread, spread.T, to_site, to_site.T, mirrored, flip)
    return [jnp.asarray(part, jnp.bfloat16) for part in parts]


def product(left, right, dims=((1,), (0,))):
    return lax.dot_general(left, right, (dims, ((), ())), preferred_element_type=jnp.float32)


def short(x):
    return x.astype(jnp.bfloat16)


def kernel(
    n,
    block,
    history,
    spread,
    gather,
    to_momentum,
    to_site,
    to_mirror,
    flip,
    out,
    outgoing,
    incoming,
    right_side,
    send_sem,
    recv_sem,
):
    q = WIDE // n
    half = 2 * q
    place = {"kx": lax.axis_index("kx"), "ky": lax.axis_index("ky")}
    barrier = pltpu.get_barrier_semaphore()

    @pl.loop(1, n)
    def _(step):
        for axis in ("kx", "ky"):
            peer = lax.rem(place[axis] + step, n)
            pl.semaphore_signal(
                barrier, inc=1, device_id={axis: peer}, device_id_type=pl.DeviceIdType.MESH
            )

    def post(slot, kinds):
        tiles = [part.reshape(n, half, WIDE) for part in kinds]
        outgoing[slot] = short(jnp.concatenate(tiles, 1))

    def launch(slot, axis):
        me = place[axis]

        @pl.loop(1, n)
        def _(step):
            far = n // 2 - step // 2 + lax.rem(step, 2) * (2 * (step // 2))
            peer = lax.rem(me + far, n)
            pltpu.make_async_remote_copy(
                src_ref=outgoing.at[slot, peer],
                dst_ref=incoming.at[slot, me],
                send_sem=send_sem.at[slot],
                recv_sem=recv_sem.at[slot],
                device_id={axis: peer},
                device_id_type=pl.DeviceIdType.MESH,
            ).start()

        incoming[slot, me] = outgoing[slot, me]

    def everything(slot, axis):
        return pltpu.make_async_remote_copy(
            src_ref=outgoing.at[slot, pl.ds(0, n - 1)],
            dst_ref=incoming.at[slot, pl.ds(0, n - 1)],
            send_sem=send_sem.at[slot],
            recv_sem=recv_sem.at[slot],
            device_id={axis: lax.rem(place[axis] + 1, n)},
            device_id_type=pl.DeviceIdType.MESH,
        )

    def take(slot, axis):
        everything(slot, axis).wait_recv()
        tiles = incoming[slot].astype(jnp.float32)
        return [
            short(tiles[:, kind * half : (kind + 1) * half].reshape(2 * WIDE, WIDE))
            for kind in range(2)
        ]

    def exchange(slot, axis, kinds):
        post(slot, kinds)
        launch(slot, axis)
        return take(slot, axis)

    def stacked(wide):
        return jnp.concatenate((wide[:, :WIDE], wide[:, WIDE:]), 0)

    def side_by_side(tall):
        return jnp.concatenate((tall[:WIDE], tall[WIDE:]), 1)

    for kind in range(2):
        for part in range(2):
            piece = history[kind, part]
            rows, lanes = kind * 2 * WIDE, part * WIDE
            right_side[rows : rows + WIDE, lanes : lanes + WIDE] = piece
            other = (1 - part) * WIDE
            turned = piece if part == 0 else -piece
            right_side[rows + WIDE : rows + 2 * WIDE, other : other + WIDE] = turned
    for part in range(2):
        piece = history[0, part].astype(jnp.float32).T
        adjoint = short(piece if part == 0 else -piece)
        rows, lanes = 4 * WIDE, part * WIDE
        right_side[rows : rows + WIDE, lanes : lanes + WIDE] = adjoint
        other = (1 - part) * WIDE
        turned = adjoint if part == 0 else -adjoint
        right_side[rows + WIDE : rows + 2 * WIDE, other : other + WIDE] = turned

    start = [block[kind].reshape(2 * WIDE, WIDE) for kind in range(2)]
    current = start
    for iteration in range(ITERS):
        slot = iteration * PHASES
        post(slot, [product(spread[...], current[kind]) for kind in range(2)])
        if iteration == 0:
            pl.semaphore_wait(barrier, 2 * (n - 1))
        launch(slot, "kx")
        rows_in = take(slot, "kx")
        half_way = []
        for kind in range(2):
            turned = product(rows_in[kind], to_momentum[...], ((0,), (0,)))
            half_way.append(product(spread[...], short(stacked(turned))))
        columns_in = exchange(slot + 1, "ky", half_way)
        green, mirror = [], []
        for kind in range(2):
            site = product(to_site[...], columns_in[kind])
            green.append((site[:WIDE], site[WIDE:]))
            flipped = short(product(columns_in[kind], flip[...]))
            site = product(to_mirror[...], flipped)
            mirror.append((site[:WIDE], site[WIDE:]))
        selves = []
        for kind in range(2):
            real, imag = green[kind]
            other_real, other_imag = mirror[1 - kind]
            square_real = real * real - imag * imag
            square_imag = real * imag + imag * real
            self_real = square_real * other_real + square_imag * other_imag
            self_imag = square_imag * other_real - square_real * other_imag
            selves.append(short(jnp.concatenate((self_real, self_imag), 0)))
        half_back = exchange(
            slot + 2, "ky", [product(to_momentum[...], selves[kind]) for kind in range(2)]
        )
        last = []
        for kind in range(2):
            regrouped = side_by_side(short(product(gather[...], half_back[kind])))
            last.append(product(to_momentum[...], regrouped, ((1,), (1,))))
        whole = exchange(slot + 3, "kx", last)
        sides = [
            side_by_side(short(product(gather[...], whole[kind]))) for kind in range(2)
        ]
        retarded = product(sides[0], right_side[0 : 2 * WIDE])
        lesser = product(
            jnp.concatenate(sides, 1), right_side[2 * WIDE : 6 * WIDE]
        )
        collision = [stacked(retarded), stacked(lesser)]
        if iteration + 1 < ITERS:
            current = [
                short(start[kind].astype(jnp.float32) + coupling * collision[kind])
                for kind in range(2)
            ]
    for kind in range(2):
        out[kind] = collision[kind].reshape(2, WIDE, WIDE)
    for slot in range(ITERS * PHASES):
        axis = "kx" if slot % PHASES in (0, 3) else "ky"
        everything(slot, axis).wait_send()


def solution(mesh):
    n = mesh.shape["kx"]
    slots = ITERS * PHASES
    spec = P("kx", "ky", None, None, None, None)

    def on_device(block, history):
        result = pl.pallas_call(
            lambda *refs: kernel(n, *refs),
            out_shape=jax.ShapeDtypeStruct((2, 2, WIDE, WIDE), jnp.float32),
            in_specs=[pl.BlockSpec(memory_space=pltpu.VMEM)] * 8,
            out_specs=pl.BlockSpec(memory_space=pltpu.VMEM),
            scratch_shapes=[
                pltpu.VMEM((slots, n, 4 * WIDE // n, WIDE), jnp.bfloat16),
                pltpu.VMEM((slots, n, 4 * WIDE // n, WIDE), jnp.bfloat16),
                pltpu.VMEM((6 * WIDE, 2 * WIDE), jnp.bfloat16),
                pltpu.SemaphoreType.DMA((slots,)),
                pltpu.SemaphoreType.DMA((slots,)),
            ],
            compiler_params=pltpu.CompilerParams(collective_id=0, has_side_effects=True),
        )(block[0, 0], history[0, 0], *tables(n))
        return result[None, None]

    return jax.shard_map(
        on_device, mesh=mesh, in_specs=(spec, spec), out_specs=spec, check_vma=False
    )
```

```python
import math

import jax
import jax.numpy as jnp
import numpy as np
from jax import lax
from jax.experimental import pallas as pl
from jax.experimental.pallas import tpu as pltpu
from jax.sharding import PartitionSpec as P

ITERS = 2
PHASES = 4
CHUNKS = 2
WIDE = 128
STRETCH = 1.62175

coupling = 0.5


def tables(n):
    q = WIDE // n
    part = q // CHUNKS
    unit = np.eye(2 * WIDE, dtype=np.float32)
    spread = unit.reshape(2, q, n, -1).transpose(2, 0, 1, 3).reshape(2 * WIDE, -1)
    first = unit.reshape(4, part, n, -1).transpose(2, 0, 1, 3).reshape(2 * WIDE, -1)
    phases = np.outer(np.arange(n), np.arange(n)) % n * (2.0 * math.pi / n)
    cosine = np.cos(phases)
    sine = np.sin(phases)
    mixed = np.stack((np.stack((cosine, sine), 1), np.stack((-sine, cosine), 1)), 1)
    along_y = np.einsum("kcdx,ij->kcidxj", mixed, np.eye(q)).reshape(2 * WIDE, 2 * WIDE)
    along_x = np.einsum(
        "kcdx,ij,st->kscidtxj", mixed, np.eye(part), np.eye(2)
    ).reshape(2 * WIDE, 2 * WIDE)
    back = (-np.arange(n)) % n
    mirrored = along_y.T.reshape(2, n, q, 2 * WIDE)[:, back].reshape(2 * WIDE, 2 * WIDE)
    flip = np.einsum(
        "st,xy,ij->sxityj", np.eye(2)[::-1], np.eye(n)[back], np.eye(part)
    ).reshape(WIDE, WIDE)

    def scaled(table):
        return jnp.asarray(table * STRETCH, jnp.bfloat16)

    held = (cosine * STRETCH).astype(jnp.bfloat16).astype(np.float64)
    factor = float((held * cosine).sum() / (held * held).sum() / math.sqrt(n))
    exact = [jnp.asarray(table, jnp.bfloat16) for table in (spread, spread.T, first, first.T, flip)]
    return factor, exact + [scaled(t) for t in (along_x, along_y, along_y.T, mirrored)]


def product(left, right, dims=((1,), (0,))):
    return lax.dot_general(left, right, (dims, ((), ())), preferred_element_type=jnp.float32)


def short(x):
    return x.astype(jnp.bfloat16)


def kernel(
    n,
    factor,
    block,
    history,
    spread,
    gather,
    first_spread,
    first_gather,
    flip,
    along_x,
    along_y,
    to_site,
    to_mirror,
    out,
    outgoing,
    incoming,
    right_side,
    send_sem,
    recv_sem,
):
    rows = WIDE // CHUNKS
    place = {"kx": lax.axis_index("kx"), "ky": lax.axis_index("ky")}
    barrier = pltpu.get_barrier_semaphore()

    @pl.loop(1, n)
    def _(step):
        for axis in ("kx", "ky"):
            peer = lax.rem(place[axis] + step, n)
            pl.semaphore_signal(
                barrier, inc=1, device_id={axis: peer}, device_id_type=pl.DeviceIdType.MESH
            )

    def axis_of(slot):
        return "kx" if slot // CHUNKS % PHASES in (0, 3) else "ky"

    def post(slot, tall):
        outgoing[slot] = short(tall.reshape(outgoing.shape[1:]))

    def launch(slot):
        axis = axis_of(slot)
        me = place[axis]

        @pl.loop(1, n)
        def _(step):
            far = n // 2 - step // 2 + lax.rem(step, 2) * (2 * (step // 2))
            peer = lax.rem(me + far, n)
            pltpu.make_async_remote_copy(
                src_ref=outgoing.at[slot, peer],
                dst_ref=incoming.at[slot, me],
                send_sem=send_sem.at[slot],
                recv_sem=recv_sem.at[slot],
                device_id={axis: peer},
                device_id_type=pl.DeviceIdType.MESH,
            ).start()

        incoming[slot, me] = outgoing[slot, me]

    def everything(slot):
        axis = axis_of(slot)
        return pltpu.make_async_remote_copy(
            src_ref=outgoing.at[slot, pl.ds(0, n - 1)],
            dst_ref=incoming.at[slot, pl.ds(0, n - 1)],
            send_sem=send_sem.at[slot],
            recv_sem=recv_sem.at[slot],
            device_id={axis: lax.rem(place[axis] + 1, n)},
            device_id_type=pl.DeviceIdType.MESH,
        )

    def take(slot):
        everything(slot).wait_recv()
        return short(incoming[slot].astype(jnp.float32).reshape(2 * WIDE, WIDE))

    def stacked(wide):
        return jnp.concatenate((wide[:, :WIDE], wide[:, WIDE:]), 0)

    def side_by_side(tall):
        return jnp.concatenate((tall[:WIDE], tall[WIDE:]), 1)

    def rows_of(chunk):
        return [
            block[kind, part, chunk * rows : (chunk + 1) * rows]
            for kind in range(2)
            for part in range(2)
        ]

    def leave(chunk, received):
        turned = product(received, along_x[...], ((0,), (0,))) * factor
        return product(spread[...], short(stacked(turned)))

    def at_sites(chunk, received):
        site = product(to_site[...], received) * factor
        flipped = short(product(received, flip[...]))
        other = product(to_mirror[...], flipped) * factor
        real, imag = site[:WIDE], site[WIDE:]
        other_real, other_imag = other[:WIDE], other[WIDE:]
        square_real = real * real - imag * imag
        square_imag = real * imag + imag * real
        self_real = square_real * other_real + square_imag * other_imag
        self_imag = square_imag * other_real - square_real * other_imag
        selves = short(jnp.concatenate((self_real, self_imag), 0))
        return product(along_y[...], selves) * factor

    def come_back(chunk, received):
        regrouped = side_by_side(short(product(gather[...], received)))
        return product(along_x[...], regrouped, ((1,), (1,))) * factor

    def collide(chunk, received):
        whole = short(product(first_gather[...], received))
        sides = [whole[index * rows : (index + 1) * rows] for index in range(4)]
        retarded = product(jnp.concatenate(sides[:2], 1), right_side[0 : 2 * WIDE])
        lesser = product(jnp.concatenate(sides, 1), right_side[2 * WIDE : 6 * WIDE])
        return [
            result[:, part * WIDE : (part + 1) * WIDE]
            for result in (retarded, lesser)
            for part in range(2)
        ]

    def renew(chunk, received):
        collision = collide(chunk, received)
        current = [
            short(old.astype(jnp.float32) + coupling * new)
            for old, new in zip(rows_of(chunk), collision)
        ]
        return product(first_spread[...], jnp.concatenate(current, 0))

    for chunk in range(CHUNKS):
        post(chunk, product(first_spread[...], jnp.concatenate(rows_of(chunk), 0)))
    pl.semaphore_wait(barrier, 2 * (n - 1))
    for chunk in range(CHUNKS):
        launch(chunk)

    for kind in range(2):
        for part in range(2):
            piece = history[kind, part]
            top, lanes = kind * 2 * WIDE, part * WIDE
            right_side[top : top + WIDE, lanes : lanes + WIDE] = piece
            other = (1 - part) * WIDE
            turned = piece if part == 0 else -piece
            right_side[top + WIDE : top + 2 * WIDE, other : other + WIDE] = turned
    for part in range(2):
        piece = history[0, part].astype(jnp.float32).T
        adjoint = short(piece if part == 0 else -piece)
        top, lanes = 4 * WIDE, part * WIDE
        right_side[top : top + WIDE, lanes : lanes + WIDE] = adjoint
        other = (1 - part) * WIDE
        turned = adjoint if part == 0 else -adjoint
        right_side[top + WIDE : top + 2 * WIDE, other : other + WIDE] = turned

    steps = ITERS * (leave, at_sites, come_back, renew)
    for phase in range(ITERS * PHASES - 1):
        for chunk in range(CHUNKS):
            slot = phase * CHUNKS + chunk
            post(slot + CHUNKS, steps[phase](chunk, take(slot)))
            launch(slot + CHUNKS)
    for chunk in range(CHUNKS):
        collision = collide(chunk, take((ITERS * PHASES - 1) * CHUNKS + chunk))
        for index in range(4):
            out[index // 2, index % 2, chunk * rows : (chunk + 1) * rows] = collision[index]
    for slot in range(ITERS * PHASES * CHUNKS):
        everything(slot).wait_send()


def solution(mesh):
    n = mesh.shape["kx"]
    slots = ITERS * PHASES * CHUNKS
    tiles = (slots, n, 2 * WIDE // n, WIDE)
    spec = P("kx", "ky", None, None, None, None)

    def on_device(block, history):
        factor, held = tables(n)
        result = pl.pallas_call(
            lambda *refs: kernel(n, factor, *refs),
            out_shape=jax.ShapeDtypeStruct((2, 2, WIDE, WIDE), jnp.float32),
            in_specs=[pl.BlockSpec(memory_space=pltpu.VMEM)] * (2 + len(held)),
            out_specs=pl.BlockSpec(memory_space=pltpu.VMEM),
            scratch_shapes=[
                pltpu.VMEM(tiles, jnp.bfloat16),
                pltpu.VMEM(tiles, jnp.bfloat16),
                pltpu.VMEM((6 * WIDE, 2 * WIDE), jnp.bfloat16),
                pltpu.SemaphoreType.DMA((slots,)),
                pltpu.SemaphoreType.DMA((slots,)),
            ],
            compiler_params=pltpu.CompilerParams(collective_id=0, has_side_effects=True),
        )(block[0, 0], history[0, 0], *held)
        return result[None, None]

    return jax.shard_map(
        on_device, mesh=mesh, in_specs=(spec, spec), out_specs=spec, check_vma=False
    )
```

```python
import math

import jax
import jax.numpy as jnp
import numpy as np
from jax import lax
from jax.experimental import pallas as pl
from jax.experimental.pallas import tpu as pltpu
from jax.sharding import PartitionSpec as P

ITERS = 2
PHASES = 4
CHUNKS = 2
WIDE = 128
STRETCH = 1.62175

coupling = 0.5


def tables(n):
    q = WIDE // n
    part = q // CHUNKS
    unit = np.eye(2 * WIDE, dtype=np.float32)
    spread = unit.reshape(2, q, n, -1).transpose(2, 0, 1, 3).reshape(2 * WIDE, -1)
    first = unit.reshape(4, part, n, -1).transpose(2, 0, 1, 3).reshape(2 * WIDE, -1)
    phases = np.outer(np.arange(n), np.arange(n)) % n * (2.0 * math.pi / n)
    cosine = np.cos(phases)
    sine = np.sin(phases)
    mixed = np.stack((np.stack((cosine, sine), 1), np.stack((-sine, cosine), 1)), 1)
    along_y = np.einsum("kcdx,ij->kcidxj", mixed, np.eye(q)).reshape(2 * WIDE, 2 * WIDE)
    along_x = np.einsum(
        "kcdx,ij,st->kscidtxj", mixed, np.eye(part), np.eye(2)
    ).reshape(2 * WIDE, 2 * WIDE)
    back = (-np.arange(n)) % n
    mirrored = along_y.T.reshape(2, n, q, 2 * WIDE)[:, back].reshape(2 * WIDE, 2 * WIDE)
    flip = np.einsum(
        "st,xy,ij->sxityj", np.eye(2)[::-1], np.eye(n)[back], np.eye(part)
    ).reshape(WIDE, WIDE)

    def scaled(table):
        return jnp.asarray(table * STRETCH, jnp.bfloat16)

    held = (cosine * STRETCH).astype(jnp.bfloat16).astype(np.float64)
    factor = float((held * cosine).sum() / (held * held).sum() / math.sqrt(n))
    def plain(table):
        return jnp.asarray(table, jnp.bfloat16)

    before = [plain(first)]
    after = [scaled(along_x), plain(spread), scaled(along_y.T), plain(flip)]
    after += [scaled(mirrored), scaled(along_y), plain(spread.T), plain(first.T)]
    return factor, before, after


def product(left, right, dims=((1,), (0,))):
    return lax.dot_general(left, right, (dims, ((), ())), preferred_element_type=jnp.float32)


def short(x):
    return x.astype(jnp.bfloat16)


def kernel(
    n,
    factor,
    count,
    *refs,
):
    sources, out, held = refs[:count], refs[count], refs[count + 1 : 2 * count + 1]
    outgoing, incoming, right_side, send_sem, recv_sem, load_sem = refs[2 * count + 1 :]
    block, first_spread, history, along_x, spread, to_site, flip = held[:7]
    to_mirror, along_y, gather, first_gather = held[7:]
    rows = WIDE // CHUNKS
    place = {"kx": lax.axis_index("kx"), "ky": lax.axis_index("ky")}
    barrier = pltpu.get_barrier_semaphore()

    @pl.loop(1, n)
    def _(step):
        for axis in ("kx", "ky"):
            peer = lax.rem(place[axis] + step, n)
            pl.semaphore_signal(
                barrier, inc=1, device_id={axis: peer}, device_id_type=pl.DeviceIdType.MESH
            )

    loads = [
        pltpu.make_async_copy(source, target, load_sem.at[index])
        for index, (source, target) in enumerate(zip(sources, held))
    ]
    for load in loads:
        load.start()

    def axis_of(slot):
        outer = slot // CHUNKS % PHASES in (0, 3)
        return "kx" if outer == (slot % CHUNKS == 0) else "ky"

    def post(slot, tall):
        outgoing[slot] = short(tall.reshape(outgoing.shape[1:]))

    def launch(slot):
        axis = axis_of(slot)
        me = place[axis]

        def send(away):
            peer = lax.rem(me + away, n)
            pltpu.make_async_remote_copy(
                src_ref=outgoing.at[slot, peer],
                dst_ref=incoming.at[slot, me],
                send_sem=send_sem.at[slot],
                recv_sem=recv_sem.at[slot],
                device_id={axis: peer},
                device_id_type=pl.DeviceIdType.MESH,
            ).start()

        send(n // 4)
        send(n - n // 4)

        @pl.loop(1, n // 4)
        def _(step):
            ring = n // 4 - step
            send(n // 2 - ring)
            send(n // 2 + ring)
            send(ring)
            send(n - ring)

        send(n // 2)
        incoming[slot, me] = outgoing[slot, me]

    def everything(slot):
        axis = axis_of(slot)
        return pltpu.make_async_remote_copy(
            src_ref=outgoing.at[slot, pl.ds(0, n - 1)],
            dst_ref=incoming.at[slot, pl.ds(0, n - 1)],
            send_sem=send_sem.at[slot],
            recv_sem=recv_sem.at[slot],
            device_id={axis: lax.rem(place[axis] + 1, n)},
            device_id_type=pl.DeviceIdType.MESH,
        )

    def take(slot):
        everything(slot).wait_recv()
        return short(incoming[slot].astype(jnp.float32).reshape(2 * WIDE, WIDE))

    def stacked(wide):
        return jnp.concatenate((wide[:, :WIDE], wide[:, WIDE:]), 0)

    def side_by_side(tall):
        return jnp.concatenate((tall[:WIDE], tall[WIDE:]), 1)

    def rows_of(chunk):
        return [
            block[kind, part, chunk * rows : (chunk + 1) * rows]
            for kind in range(2)
            for part in range(2)
        ]

    def leave(chunk, received):
        turned = product(received, along_x[...], ((0,), (0,))) * factor
        return product(spread[...], short(stacked(turned)))

    def at_sites(chunk, received):
        site = product(to_site[...], received) * factor
        flipped = short(product(received, flip[...]))
        other = product(to_mirror[...], flipped) * factor
        real, imag = site[:WIDE], site[WIDE:]
        other_real, other_imag = other[:WIDE], other[WIDE:]
        square_real = real * real - imag * imag
        square_imag = real * imag + imag * real
        self_real = square_real * other_real + square_imag * other_imag
        self_imag = square_imag * other_real - square_real * other_imag
        selves = short(jnp.concatenate((self_real, self_imag), 0))
        return product(along_y[...], selves) * factor

    def come_back(chunk, received):
        regrouped = side_by_side(short(product(gather[...], received)))
        return product(along_x[...], regrouped, ((1,), (1,))) * factor

    def collide(chunk, received):
        whole = short(product(first_gather[...], received))
        sides = [whole[index * rows : (index + 1) * rows] for index in range(4)]
        retarded = product(jnp.concatenate(sides[:2], 1), right_side[0 : 2 * WIDE])
        lesser = product(jnp.concatenate(sides, 1), right_side[2 * WIDE : 6 * WIDE])
        return [
            result[:, part * WIDE : (part + 1) * WIDE]
            for result in (retarded, lesser)
            for part in range(2)
        ]

    def renew(chunk, received):
        collision = collide(chunk, received)
        current = [
            short(old.astype(jnp.float32) + coupling * new)
            for old, new in zip(rows_of(chunk), collision)
        ]
        return product(first_spread[...], jnp.concatenate(current, 0))

    for load in loads[:2]:
        load.wait()
    for chunk in range(CHUNKS):
        post(chunk, product(first_spread[...], jnp.concatenate(rows_of(chunk), 0)))
    pl.semaphore_wait(barrier, 2 * (n - 1))
    for chunk in range(CHUNKS):
        launch(chunk)
    for load in loads[2:]:
        load.wait()

    for kind in range(2):
        for part in range(2):
            piece = history[kind, part]
            top, lanes = kind * 2 * WIDE, part * WIDE
            right_side[top : top + WIDE, lanes : lanes + WIDE] = piece
            other = (1 - part) * WIDE
            turned = piece if part == 0 else -piece
            right_side[top + WIDE : top + 2 * WIDE, other : other + WIDE] = turned
    for part in range(2):
        piece = history[0, part].astype(jnp.float32).T
        adjoint = short(piece if part == 0 else -piece)
        top, lanes = 4 * WIDE, part * WIDE
        right_side[top : top + WIDE, lanes : lanes + WIDE] = adjoint
        other = (1 - part) * WIDE
        turned = adjoint if part == 0 else -adjoint
        right_side[top + WIDE : top + 2 * WIDE, other : other + WIDE] = turned

    steps = ITERS * (leave, at_sites, come_back, renew)
    for phase in range(ITERS * PHASES - 1):
        for chunk in range(CHUNKS):
            slot = phase * CHUNKS + chunk
            post(slot + CHUNKS, steps[phase](chunk, take(slot)))
            launch(slot + CHUNKS)
    for chunk in range(CHUNKS):
        collision = collide(chunk, take((ITERS * PHASES - 1) * CHUNKS + chunk))
        for index in range(4):
            out[index // 2, index % 2, chunk * rows : (chunk + 1) * rows] = collision[index]
    for slot in range(ITERS * PHASES * CHUNKS):
        everything(slot).wait_send()


def solution(mesh):
    n = mesh.shape["kx"]
    slots = ITERS * PHASES * CHUNKS
    tiles = (slots, n, 2 * WIDE // n, WIDE)
    spec = P("kx", "ky", None, None, None, None)

    def on_device(block, history):
        factor, before, after = tables(n)
        operands = [block[0, 0], *before, history[0, 0], *after]
        result = pl.pallas_call(
            lambda *refs: kernel(n, factor, len(operands), *refs),
            out_shape=jax.ShapeDtypeStruct((2, 2, WIDE, WIDE), jnp.float32),
            in_specs=[pl.BlockSpec(memory_space=pl.ANY)] * len(operands),
            out_specs=pl.BlockSpec(memory_space=pltpu.VMEM),
            scratch_shapes=[pltpu.VMEM(part.shape, part.dtype) for part in operands]
            + [
                pltpu.VMEM(tiles, jnp.bfloat16),
                pltpu.VMEM(tiles, jnp.bfloat16),
                pltpu.VMEM((6 * WIDE, 2 * WIDE), jnp.bfloat16),
                pltpu.SemaphoreType.DMA((slots,)),
                pltpu.SemaphoreType.DMA((slots,)),
                pltpu.SemaphoreType.DMA((len(operands),)),
            ],
            compiler_params=pltpu.CompilerParams(collective_id=0, has_side_effects=True),
        )(*operands)
        return result[None, None]

    return jax.shard_map(
        on_device, mesh=mesh, in_specs=(spec, spec), out_specs=spec, check_vma=False
    )
```
